32 devices in a mesh: virt: 2 (over y), occ: 4 (over z), aux: 4 (over x, core).
Axes of the slice: x: 2, y: 2, z: 4, core: 2. Of those that a mesh axis runs over, the one named last changes fastest.
Arguments:
- three_index: bfloat16 [16384, 4, 1536], P('aux', 'occ', 'virt'), may hold values from -0.59765625 to 0.59765625
- occupied_energy: bfloat16 [4], P('occ'), may hold values from -2 to -0.5
- virtual_energy: float32 [1536], P('virt'), may hold values from 0.2 to 3
Outputs:
- density: bfloat16 [16384, 4, 1536], P('aux', 'occ', 'virt')
The draws below stay inside these ranges and needn't reach their ends.
All inputs are finite; a program needn't handle non-finite values.
Results may differ from the reference program's by a relative error of at most 0.0046.
Values may be sent and summed in bfloat16 or wider, within the bound.
A program may use at most 128 MiB of HBM per device.

```python
import math
import jax
import jax.numpy as jnp
from jax import lax

NAUX = 16384
VS = 768
OCC_DEV = 1
NOCC = 4
NVIRT = 1536
N_VIRT = 2
N_OCC = 4


def shard_levels(stream_key, shape, cuts, smallest, high):
    level = 1.0
    for dim, parts in cuts:
        draws = jax.random.uniform(jax.random.fold_in(jax.random.fold_in(stream_key, 6), dim), (parts,), jnp.float32, smallest / len(cuts), high / len(cuts))
        level = level * jnp.repeat(jnp.exp(draws), shape[dim] // parts).reshape((-1,) + (1,) * (len(shape) - 1 - dim))
    return level


def bell_draw(rng, dims, spread, reach, shards=(), kind=jnp.bfloat16):
    level = shard_levels(rng, dims, shards, -0.22, 0.18) if shards else 1.0
    entries = jax.random.normal(rng, dims, jnp.float32) * spread * level
    return jnp.minimum(jnp.maximum(entries, -reach), reach).astype(kind)


def setup_inputs(seed: int = 0) -> dict:
    seeds = jax.random.split(jax.random.key(seed), 4)
    three_index = bell_draw(seeds[0], (NAUX, NOCC, NVIRT), 0.1, 0.59765625, ((0, 4), (1, 4), (2, 2)))
    occupied_energy = jnp.clip(-2.0 + 1.5 * jax.random.uniform(seeds[1], (NOCC,), jnp.float32) ** shard_levels(seeds[1], (NOCC,), ((0, 4),), -0.2, 0.2), -2.0, -0.5).astype(jnp.bfloat16)
    virtual_energy = jnp.clip(jnp.exp(math.log(3.0) - 2.7080502 * jax.random.uniform(seeds[2], (NVIRT,), jnp.float32) ** shard_levels(seeds[2], (NVIRT,), ((0, 2),), -0.2, 0.2)), 0.2, 3.0)
    return dict(three_index=three_index, occupied_energy=occupied_energy, virtual_energy=virtual_energy)


spin_scale = 1.2


def pair_amplitudes(left_block, right_block, left_occupied, right_occupied, virtual_slab):
    pair_sums = lax.dot_general(left_block, right_block, (((0,), (0,)), ((), ())), preferred_element_type=jnp.float32)
    left_levels = (virtual_slab[None, :] - left_occupied.astype(jnp.float32)[:, None]).reshape(-1)
    right_levels = (virtual_slab[None, :] - right_occupied.astype(jnp.float32)[:, None]).reshape(-1)
    denominator = left_levels[:, None] + right_levels[None, :]
    return (spin_scale * pair_sums / denominator).astype(jnp.bfloat16)


def reference(three_index, occupied_energy, virtual_energy):
    blocks = three_index.reshape(NAUX, N_OCC, OCC_DEV, N_VIRT, VS)
    energies = occupied_energy.reshape(N_OCC, OCC_DEV)
    results = []
    for group in range(N_VIRT):
        slab_blocks = jnp.transpose(blocks[:, :, :, group, :].reshape(NAUX, N_OCC, OCC_DEV * VS), (1, 0, 2))
        virtual_slab = virtual_energy[group * VS:(group + 1) * VS]

        def visit(position, accumulated):
            position = jnp.asarray(position).astype(jnp.int32)
            for offset in (1, 2):
                partner = ((position - offset) % N_OCC).astype(jnp.int32)
                left_block = slab_blocks[position]
                right_block = slab_blocks[partner]
                amplitude = pair_amplitudes(left_block, right_block, energies[position], energies[partner], virtual_slab)
                own_term = lax.dot_general(right_block, amplitude, (((1,), (1,)), ((), ())), preferred_element_type=jnp.float32)
                partner_term = jnp.dot(left_block, amplitude, preferred_element_type=jnp.float32)
                accumulated = accumulated.at[position].add(own_term)
                accumulated = accumulated.at[partner].add(partner_term)
            return accumulated

        accumulated = lax.fori_loop(0, N_OCC, visit, jnp.zeros((N_OCC, NAUX, OCC_DEV * VS), jnp.float32))
        rounded = accumulated.astype(jnp.bfloat16)
        results.append(jnp.transpose(rounded, (1, 0, 2)).reshape(NAUX, N_OCC, OCC_DEV, VS))
    stacked = jnp.stack(results, axis=3)
    return stacked.reshape(NAUX, N_OCC * OCC_DEV, N_VIRT * VS)
```

```python
import functools

import jax
import jax.numpy as jnp
from jax import lax
from jax.experimental import pallas as pl
from jax.experimental.pallas import tpu as pltpu
from jax.sharding import PartitionSpec as P

spin_scale = 1.2
MESH = pl.DeviceIdType.MESH
CHUNKS = 8
WIDE = 256
F32, BF16 = jnp.float32, jnp.bfloat16


def shifted(block, axis, distance):
    devices = range(lax.axis_size(axis))
    route = [((i - distance) % len(devices), i) for i in devices]
    return lax.ppermute(block, axis, route)


def level_matrix(virtual_energy, left_occupied, right_occupied):
    left_levels = (virtual_energy[None, :] - left_occupied.astype(jnp.float32)[:, None]).reshape(-1)
    right_levels = (virtual_energy[None, :] - right_occupied.astype(jnp.float32)[:, None]).reshape(
        -1
    )
    return left_levels[:, None] + right_levels[None, :]


def amplitudes(own_block, far_block, own_energy, far_energy, virtual_energy):
    partial_sums = lax.dot_general(
        own_block, far_block, (((0,), (0,)), ((), ())), preferred_element_type=jnp.float32
    )
    pair_sums = lax.psum(partial_sums, "aux")
    denominator = level_matrix(virtual_energy, own_energy, far_energy)
    return (spin_scale * pair_sums / denominator).astype(jnp.bfloat16)


def any_cycle(three_index, occupied_energy, virtual_energy):
    aux_rows, occ_rows, slab_size = three_index.shape
    own_block = three_index.reshape(aux_rows, occ_rows * slab_size)
    first_index, first_energy = shifted((three_index, occupied_energy), "occ", 1)
    second_index, second_energy = shifted((first_index, first_energy), "occ", 1)
    first_block = first_index.reshape(aux_rows, occ_rows * slab_size)
    second_block = second_index.reshape(aux_rows, occ_rows * slab_size)
    later_one = shifted(own_block, "occ", -1)
    later_two = shifted(own_block, "occ", -2)
    first_amplitude = amplitudes(
        own_block, first_block, occupied_energy, first_energy, virtual_energy
    )
    accumulated = lax.dot_general(
        first_block, first_amplitude, (((1,), (1,)), ((), ())), preferred_element_type=jnp.float32
    )
    arrived_one = shifted(first_amplitude, "occ", -1)
    accumulated = accumulated + jnp.dot(later_one, arrived_one, preferred_element_type=jnp.float32)
    second_amplitude = amplitudes(
        own_block, second_block, occupied_energy, second_energy, virtual_energy
    )
    accumulated = accumulated + lax.dot_general(
        second_block, second_amplitude, (((1,), (1,)), ((), ())), preferred_element_type=jnp.float32
    )
    arrived_two = shifted(second_amplitude, "occ", -2)
    accumulated = accumulated + jnp.dot(later_two, arrived_two, preferred_element_type=jnp.float32)
    return accumulated.astype(jnp.bfloat16).reshape(aux_rows, occ_rows, slab_size)


OI, OJ, IJ, OK = range(4)


def four_blocks(x, e_own, e_row, e_col, out, o_buf, j_buf, k_buf, stage_o, stage_i, g, t, t_ki,
                z_out, z_in, c_out, c_in, x_out, x_in, e_buf,
                o_s, o_r, j_s, j_r, k_s, k_r, res_s, res_r, e_s, e_r, z_s, z_r,
                c_s, c_r, x_s, x_r, t_s, t_r, ki_s, ki_r, out_s):
    rows, width = x.shape
    size, half = rows // CHUNKS, width // 2
    v, z, a = lax.axis_index("virt"), lax.axis_index("occ"), lax.axis_index("aux")
    core = lax.rem(a, 2)
    inner = jnp.logical_or(z == 1, z == 2)
    outer = jnp.logical_or(z == 0, z == 3)
    mate_z = z + 1 - 2 * lax.rem(z, 2)
    mate, mirror = (v, mate_z, a), (v, 3 - z, a)
    core_mate, x_mate = (v, z, a + 1 - 2 * core), (v, z, lax.rem(a + 2, 4))
    around = [(v, lax.rem(z + d, 4), a) for d in (1, 2, 3)]

    barrier = pltpu.get_barrier_semaphore()
    for peer in around + [core_mate, x_mate]:
        pl.semaphore_signal(barrier, inc=1, device_id=peer, device_id_type=MESH)
    pl.semaphore_wait(barrier, 5)

    def remote(src, dst, send, recv, peer):
        return pltpu.make_async_remote_copy(
            src_ref=src, dst_ref=dst, send_sem=send, recv_sem=recv, device_id=peer,
            device_id_type=MESH)

    def part(c):
        return pl.ds(pl.multiple_of(c * size, size), size)

    energies = [remote(e_own, e_buf.at[d], e_s.at[d], e_r.at[d], around[d]) for d in range(3)]
    for copy in energies:
        copy.start()

    def o_copy(c):
        return remote(x.at[part(c)], o_buf.at[part(c)], o_s.at[c], o_r.at[c], mate)

    def j_copy(c):
        return remote(x.at[part(c)], j_buf.at[part(c)], j_s.at[c], j_r.at[c], mirror)

    def k_copy(c):
        return remote(o_buf.at[part(c)], k_buf.at[part(c)], k_s.at[c], k_r.at[c], mirror)

    def res_copy(c):
        return remote(stage_o.at[lax.rem(c, 2)], o_buf.at[part(c)], res_s.at[c], res_r.at[c], mate)

    def out_copy(c):
        return pltpu.make_async_copy(stage_i.at[lax.rem(c, 2)], out.at[part(c)],
                                     out_s.at[lax.rem(c, 2)])

    def gram(pair, left, right, c):
        @pl.loop(0, width // WIDE)
        def _(n):
            cols = pl.ds(pl.multiple_of(n * WIDE, WIDE), WIDE)
            g[pair, :, cols] += lax.dot_general(
                left[part(c), :], right[part(c), cols], (((0,), (0,)), ((), ())),
                preferred_element_type=F32)

    for copy in energies:
        copy.wait()

    @pl.when(outer)
    def _():
        @pl.loop(0, CHUNKS)
        def _(c):
            o_copy(c).start()

        @pl.loop(0, CHUNKS)
        def _(c):
            res_copy(c).wait_recv()
            pltpu.make_async_copy(o_buf.at[part(c)], out.at[part(c)], out_s.at[0]).start()
            pltpu.make_async_copy(o_buf.at[part(c)], out.at[part(c)], out_s.at[0]).wait()

        @pl.loop(0, CHUNKS)
        def _(c):
            o_copy(c).wait_send()

    @pl.when(inner)
    def _():
        @pl.loop(0, CHUNKS)
        def _(c):
            j_copy(c).start()

        g[...] = jnp.zeros_like(g)

        @pl.loop(0, CHUNKS)
        def _(c):
            o_copy(c).wait_recv()
            j_copy(c).wait_recv()
            gram(OI, o_buf, x, c)
            gram(OJ, o_buf, j_buf, c)
            gram(IJ, x, j_buf, c)

        first = jnp.where(z == 1, CHUNKS // 2, 0)

        @pl.loop(0, CHUNKS)
        def _(c):
            j_copy(c).wait_send()
            k_copy(lax.rem(c + first, CHUNKS)).start()

        mine = pl.ds(pl.multiple_of(core * half, half), half)
        other = pl.ds(pl.multiple_of(half - core * half, half), half)
        e_i = e_own[0:1, 0:1]

        def occupied(block):
            slot = lax.rem(z - block + 3, 4)
            return e_buf[slot][0:1, 0:1]

        e_o, e_j, e_k = occupied(mate_z), occupied(3 - z), occupied(3 - mate_z)

        def core_copy(p):
            return remote(c_out.at[p], c_in.at[p], c_s.at[p], c_r.at[p], core_mate)

        def x_copy(p):
            return remote(x_out.at[p], x_in.at[p], x_s.at[p], x_r.at[p], x_mate)

        def t_copy(p):
            return remote(t.at[p, mine], t.at[p, mine], t_s.at[p], t_r.at[p], core_mate)

        def reduce(pairs):
            for p, _, _, _ in pairs:
                c_out[p] = g[p, other, :].astype(BF16)
                core_copy(p).start()
            for p, _, _, _ in pairs:
                core_copy(p).wait()
                x_out[p] = (g[p, mine, :] + c_in[p].astype(F32)).astype(BF16)
                x_copy(p).start()
            for p, left, right, weight in pairs:
                x_copy(p).wait()
                sums = x_out[p].astype(F32) + x_in[p].astype(F32)
                levels = (e_col[mine, :] - left) + (e_row[...] - right)
                t[p, mine, :] = ((spin_scale * sums / levels).astype(BF16).astype(F32)
                                 * weight).astype(BF16)
                t_copy(p).start()
            for p, _, _, _ in pairs:
                t_copy(p).wait()

        reduce([(OJ, e_o, e_j, 2.0), (OI, e_o, e_i, 1.0), (IJ, e_i, e_j, 1.0)])
        ki_copy = remote(t.at[OJ], t_ki, ki_s, ki_r, mirror)
        ki_copy.start()

        @pl.loop(0, CHUNKS // 2)
        def _(c):
            at = jnp.where(z == 1, c, c + CHUNKS // 2)
            k_copy(at).wait_recv()
            gram(OK, o_buf, k_buf, at)

        z_out[...] = g[OK].astype(BF16)
        z_copy = remote(z_out, z_in, z_s, z_r, mirror)
        z_copy.start()
        z_copy.wait()
        g[OK] += z_in[...].T.astype(F32)
        reduce([(OK, e_o, e_k, 1.0)])
        ki_copy.wait()

        nt = (((1,), (1,)), ((), ()))
        nn = (((1,), (0,)), ((), ()))

        def product(left, right, dims):
            return lax.dot_general(left, right, dims, preferred_element_type=F32)

        @pl.loop(0, CHUNKS)
        def _(c):
            at = jnp.where(z == 1, c, lax.rem(c + CHUNKS // 2, CHUNKS))
            before = jnp.where(z == 1, c - 2, lax.rem(c + CHUNKS // 2 - 2, CHUNKS))
            slot = lax.rem(c, 2)

            @pl.when(c >= CHUNKS // 2)
            def _():
                k_copy(at).wait_recv()

            @pl.when(c >= 2)
            def _():
                res_copy(before).wait_send()
                out_copy(before).wait()

            @pl.loop(0, width // WIDE)
            def _(n):
                cols = pl.ds(pl.multiple_of(n * WIDE, WIDE), WIDE)
                stage_o[slot, :, cols] = (
                    product(x[part(at), :], t[OI, cols, :], nt)
                    + product(j_buf[part(at), :], t[OJ, cols, :], nt)
                    + product(k_buf[part(at), :], t[OK, cols, :], nt)).astype(BF16)

            res_copy(at).start()

            @pl.loop(0, width // WIDE)
            def _(n):
                cols = pl.ds(pl.multiple_of(n * WIDE, WIDE), WIDE)
                stage_i[slot, :, cols] = (
                    product(o_buf[part(at), :], t[OI, :, cols], nn)
                    + product(j_buf[part(at), :], t[IJ, cols, :], nt)
                    + product(k_buf[part(at), :], t_ki[:, cols], nn)).astype(BF16)

            out_copy(at).start()

        @pl.loop(CHUNKS - 2, CHUNKS)
        def _(c):
            at = jnp.where(z == 1, c, lax.rem(c + CHUNKS // 2, CHUNKS))
            res_copy(at).wait_send()
            out_copy(at).wait()

        @pl.loop(0, CHUNKS)
        def _(c):
            k_copy(c).wait_send()


def cycle_of_four(three_index, occupied_energy, virtual_energy):
    rows, _, width = three_index.shape
    half = width // 2
    pair = lambda n: pltpu.SemaphoreType.DMA((n,))
    one = pltpu.SemaphoreType.DMA
    scratch = [
        pltpu.VMEM((rows, width), BF16), pltpu.VMEM((rows, width), BF16),
        pltpu.VMEM((rows, width), BF16),
        pltpu.VMEM((2, rows // CHUNKS, width), BF16), pltpu.VMEM((2, rows // CHUNKS, width), BF16),
        pltpu.VMEM((4, width, width), F32), pltpu.VMEM((4, width, width), BF16),
        pltpu.VMEM((width, width), BF16), pltpu.VMEM((width, width), BF16),
        pltpu.VMEM((width, width), BF16),
        pltpu.VMEM((4, half, width), BF16), pltpu.VMEM((4, half, width), BF16),
        pltpu.VMEM((4, half, width), BF16), pltpu.VMEM((4, half, width), BF16),
        pltpu.VMEM((3, 8, 128), F32),
        pair(CHUNKS), pair(CHUNKS), pair(CHUNKS), pair(CHUNKS), pair(CHUNKS), pair(CHUNKS),
        pair(CHUNKS), pair(CHUNKS), pair(3), pair(3), one, one,
        pair(4), pair(4), pair(4), pair(4), pair(4), pair(4), one, one, pair(2),
    ]
    vmem = pl.BlockSpec(memory_space=pltpu.VMEM)
    density = pl.pallas_call(
        four_blocks,
        out_shape=jax.ShapeDtypeStruct((rows, width), BF16),
        in_specs=[vmem] * 4,
        out_specs=pl.BlockSpec(memory_space=pl.ANY),
        scratch_shapes=scratch,
        compiler_params=pltpu.CompilerParams(
            collective_id=0, has_side_effects=True, vmem_limit_bytes=67_000_000),
    )(
        three_index.reshape(rows, width),
        jnp.broadcast_to(occupied_energy.astype(F32)[:, None], (8, 128)),
        virtual_energy[None, :],
        virtual_energy[:, None],
    )
    return density.reshape(rows, 1, width)


def solution(mesh):
    placed = (P("aux", "occ", "virt"), P("occ"), P("virt"))

    def on_device(three_index, occupied_energy, virtual_energy):
        paired = mesh.shape["occ"] == 4 and mesh.shape["aux"] == 4 and three_index.shape[1] == 1
        body = cycle_of_four if paired else any_cycle
        return body(three_index, occupied_energy, virtual_energy)

    return jax.shard_map(
        on_device, mesh=mesh, in_specs=placed, out_specs=P("aux", "occ", "virt"), check_vma=False
    )
```

```python
import functools

import jax
import jax.numpy as jnp
from jax import lax
from jax.experimental import pallas as pl
from jax.experimental.pallas import tpu as pltpu
from jax.sharding import PartitionSpec as P

spin_scale = 1.2
MESH = pl.DeviceIdType.MESH
CHUNKS = 8
WIDE = 256
F32, BF16 = jnp.float32, jnp.bfloat16


def shifted(block, axis, distance):
    devices = range(lax.axis_size(axis))
    route = [((i - distance) % len(devices), i) for i in devices]
    return lax.ppermute(block, axis, route)


def level_matrix(virtual_energy, left_occupied, right_occupied):
    left_levels = (virtual_energy[None, :] - left_occupied.astype(jnp.float32)[:, None]).reshape(-1)
    right_levels = (virtual_energy[None, :] - right_occupied.astype(jnp.float32)[:, None]).reshape(
        -1
    )
    return left_levels[:, None] + right_levels[None, :]


def amplitudes(own_block, far_block, own_energy, far_energy, virtual_energy):
    partial_sums = lax.dot_general(
        own_block, far_block, (((0,), (0,)), ((), ())), preferred_element_type=jnp.float32
    )
    pair_sums = lax.psum(partial_sums, "aux")
    denominator = level_matrix(virtual_energy, own_energy, far_energy)
    return (spin_scale * pair_sums / denominator).astype(jnp.bfloat16)


def any_cycle(three_index, occupied_energy, virtual_energy):
    aux_rows, occ_rows, slab_size = three_index.shape
    own_block = three_index.reshape(aux_rows, occ_rows * slab_size)
    first_index, first_energy = shifted((three_index, occupied_energy), "occ", 1)
    second_index, second_energy = shifted((first_index, first_energy), "occ", 1)
    first_block = first_index.reshape(aux_rows, occ_rows * slab_size)
    second_block = second_index.reshape(aux_rows, occ_rows * slab_size)
    later_one = shifted(own_block, "occ", -1)
    later_two = shifted(own_block, "occ", -2)
    first_amplitude = amplitudes(
        own_block, first_block, occupied_energy, first_energy, virtual_energy
    )
    accumulated = lax.dot_general(
        first_block, first_amplitude, (((1,), (1,)), ((), ())), preferred_element_type=jnp.float32
    )
    arrived_one = shifted(first_amplitude, "occ", -1)
    accumulated = accumulated + jnp.dot(later_one, arrived_one, preferred_element_type=jnp.float32)
    second_amplitude = amplitudes(
        own_block, second_block, occupied_energy, second_energy, virtual_energy
    )
    accumulated = accumulated + lax.dot_general(
        second_block, second_amplitude, (((1,), (1,)), ((), ())), preferred_element_type=jnp.float32
    )
    arrived_two = shifted(second_amplitude, "occ", -2)
    accumulated = accumulated + jnp.dot(later_two, arrived_two, preferred_element_type=jnp.float32)
    return accumulated.astype(jnp.bfloat16).reshape(aux_rows, occ_rows, slab_size)


OI, OJ, IJ, OK, KI = range(5)


def four_blocks(x, e_own, e_row, e_col, out, o_buf, j_buf, k_buf, stage_o, stage_i, g, t,
                z_out, z_in, c_in, x_out, x_in, e_buf,
                o_s, o_r, j_s, j_r, k_s, k_r, res_s, res_r, raw_s, raw_r, e_s, e_r, z_s, z_r,
                c_s, c_r, x_s, x_r, t_s, t_r, go_s, go_r, ki_s, ki_r, out_s):
    rows, width = x.shape
    size, half, early = rows // CHUNKS, width // 2, CHUNKS // 2
    v, z, a = lax.axis_index("virt"), lax.axis_index("occ"), lax.axis_index("aux")
    core = lax.rem(a, 2)
    inner = jnp.logical_or(z == 1, z == 2)
    outer = jnp.logical_or(z == 0, z == 3)
    mate_z = z + 1 - 2 * lax.rem(z, 2)
    mate, mirror = (v, mate_z, a), (v, 3 - z, a)
    core_mate, x_mate = (v, z, a + 1 - 2 * core), (v, z, lax.rem(a + 2, 4))
    around = [(v, lax.rem(z + d, 4), a) for d in (1, 2, 3)]
    base = early * (z // 2)

    barrier = pltpu.get_barrier_semaphore()
    for peer in around + [core_mate, x_mate]:
        pl.semaphore_signal(barrier, inc=1, device_id=peer, device_id_type=MESH)
    pl.semaphore_wait(barrier, 5)

    def remote(src, dst, send, recv, peer):
        return pltpu.make_async_remote_copy(
            src_ref=src, dst_ref=dst, send_sem=send, recv_sem=recv, device_id=peer,
            device_id_type=MESH)

    def turn(c):
        return lax.rem(c + base, CHUNKS)

    def part(at):
        return pl.ds(pl.multiple_of(at * size, size), size)

    def o_copy(at):
        return remote(x.at[part(at)], o_buf.at[part(at)], o_s.at[at], o_r.at[at], mate)

    def j_copy(at):
        return remote(x.at[part(at)], j_buf.at[part(at)], j_s.at[at], j_r.at[at], mirror)

    def k_copy(at):
        return remote(o_buf.at[part(at)], k_buf.at[part(at)], k_s.at[at], k_r.at[at], mirror)

    def raw_copy(kind, at):
        src, dst = ((x, o_buf), (j_buf, j_buf), (k_buf, k_buf))[kind]
        return remote(src.at[part(at)], dst.at[part(at)], raw_s.at[kind, at], raw_r.at[kind, at],
                      mate)

    def res_copy(at):
        return remote(stage_o.at[lax.rem(at, 2)], o_buf.at[part(at)], res_s.at[at], res_r.at[at],
                      mate)

    def out_copy(at):
        return pltpu.make_async_copy(stage_i.at[lax.rem(at, 2)], out.at[part(at)],
                                     out_s.at[lax.rem(at, 2)])

    def direct_copy(at):
        return pltpu.make_async_copy(o_buf.at[part(at)], out.at[part(at)], out_s.at[2])

    mine = pl.ds(pl.multiple_of(core * half, half), half)
    other = pl.ds(pl.multiple_of(half - core * half, half), half)

    def t_copy(p):
        return remote(t.at[p, mine], t.at[p, mine], t_s.at[p], t_r.at[p], core_mate)

    def go_copy(p):
        return remote(t.at[p, mine], t.at[p, mine], go_s.at[p], go_r.at[p], mate)

    nt = (((1,), (1,)), ((), ()))
    nn = (((1,), (0,)), ((), ()))
    tn = (((0,), (0,)), ((), ()))

    def product(left, right, dims):
        return lax.dot_general(left, right, dims, preferred_element_type=F32)

    def wide_loop(body):
        @pl.loop(0, width // WIDE)
        def _(n):
            body(pl.ds(pl.multiple_of(n * WIDE, WIDE), WIDE))

    def outer_result(stage, slot, i_block, at):
        def body(cols):
            stage[slot, :, cols] = (
                product(i_block[part(at), :], t[OI, cols, :], nt)
                + product(j_buf[part(at), :], t[OJ, cols, :], nt)
                + product(k_buf[part(at), :], t[OK, cols, :], nt)).astype(BF16)

        wide_loop(body)

    def gram(pair, left, right, at):
        def body(cols):
            g[pair, :, cols] += product(left[part(at), :], right[part(at), cols], tn)

        wide_loop(body)

    def turn_over():
        @pl.when(z >= 2)
        def _():
            t[OK] = t[OK].T

    energies = [remote(e_own, e_buf.at[d], e_s.at[d], e_r.at[d], around[d]) for d in range(3)]
    for copy in energies:
        copy.start()

    @pl.when(outer)
    def _():
        @pl.loop(0, CHUNKS)
        def _(c):
            o_copy(turn(c)).start()

        for p in (OJ, OI, OK):
            go_copy(p).wait_recv()
            t_copy(p).start()
            t_copy(p).wait()
        turn_over()

        @pl.loop(0, early)
        def _(c):
            at = turn(c)
            for kind in range(3):
                raw_copy(kind, at).wait_recv()

            @pl.when(c >= 2)
            def _():
                out_copy(turn(c - 2)).wait()

            outer_result(stage_i, lax.rem(at, 2), o_buf, at)
            out_copy(at).start()

        @pl.loop(early, CHUNKS)
        def _(c):
            res_copy(turn(c)).wait_recv()
            direct_copy(turn(c)).start()
            direct_copy(turn(c)).wait()

        @pl.loop(early - 2, early)
        def _(c):
            out_copy(turn(c)).wait()

        @pl.loop(0, CHUNKS)
        def _(c):
            o_copy(c).wait_send()

        for copy in energies:
            copy.wait()

    @pl.when(inner)
    def _():
        @pl.loop(0, CHUNKS)
        def _(c):
            j_copy(lax.rem(turn(c) + early, CHUNKS)).start()

        @pl.loop(0, early)
        def _(c):
            raw_copy(0, turn(c)).start()

        g[...] = jnp.zeros_like(g)

        @pl.loop(0, CHUNKS)
        def _(c):
            at = turn(c)
            j_copy(at).wait_recv()

            @pl.when(c < early)
            def _():
                raw_copy(1, at).start()

            o_copy(at).wait_recv()

            @pl.when(c >= early)
            def _():
                k_copy(at).start()

            gram(OI, o_buf, x, at)
            gram(OJ, o_buf, j_buf, at)
            gram(IJ, x, j_buf, at)

        for copy in energies:
            copy.wait()

        def occupied(block):
            return e_buf[lax.rem(z - block + 3, 4)][0:1, 0:1]

        e_i = e_own[0:1, 0:1]
        e_o, e_j, e_k = occupied(mate_z), occupied(3 - z), occupied(3 - mate_z)

        def core_copy(p):
            return remote(g.at[p, other], c_in.at[p], c_s.at[p], c_r.at[p], core_mate)

        def x_copy(p):
            return remote(x_out.at[p], x_in.at[p], x_s.at[p], x_r.at[p], x_mate)

        def finish(p, left, right, weight):
            x_copy(p).wait()
            sums = g[p, mine, :] + x_in[p].astype(F32)
            levels = (e_col[mine, :] - left) + (e_row[...] - right)
            t[p, mine, :] = ((spin_scale * sums / levels).astype(BF16).astype(F32)
                             * weight).astype(BF16)
            t_copy(p).start()

        for p in (OJ, OI, IJ):
            core_copy(p).start()
        for p in (OJ, OI, IJ):
            core_copy(p).wait()
            g[p, mine, :] += c_in[p]
            x_out[p] = g[p, mine, :].astype(BF16)
            x_copy(p).start()

        def far_pair(c):
            at = turn(c)
            k_copy(at).wait_recv()
            raw_copy(2, at).start()

            @pl.when(z == 1)
            def _():
                gram(OK, o_buf, k_buf, at)

            @pl.when(z == 2)
            def _():
                gram(OK, k_buf, o_buf, at)

        @pl.loop(0, early - 2)
        def _(c):
            far_pair(c)

        ki_copy = remote(t.at[OJ, mine], t.at[KI, mine], ki_s, ki_r, mirror)
        finish(OJ, e_o, e_j, 2.0)
        go_copy(OJ).start()
        ki_copy.start()
        finish(OI, e_o, e_i, 1.0)
        go_copy(OI).start()
        far_pair(early - 2)
        finish(IJ, e_i, e_j, 1.0)
        far_pair(early - 1)

        core_copy(OK).start()
        core_copy(OK).wait()
        g[OK, mine, :] += c_in[OK]
        z_out[...] = g[OK, mine, :].astype(BF16)
        z_copy = remote(z_out, z_in, z_s, z_r, mirror)
        z_copy.start()

        @pl.loop(0, early)
        def _(c):
            k_copy(turn(c)).start()

        z_copy.wait()
        g[OK, mine, :] += z_in[...].astype(F32)
        x_out[OK] = g[OK, mine, :].astype(BF16)
        x_copy(OK).start()
        ki_copy.wait()
        t_copy(KI).start()
        finish(OK, jnp.where(z == 1, e_o, e_k), jnp.where(z == 1, e_k, e_o), 1.0)
        go_copy(OK).start()
        for p in (OJ, OI, IJ, KI, OK):
            t_copy(p).wait()
        for p in (OJ, OI, OK):
            go_copy(p).wait_send()
        turn_over()

        def inner_result(at):
            slot = lax.rem(at, 2)

            def body(cols):
                stage_i[slot, :, cols] = (
                    product(o_buf[part(at), :], t[OI, :, cols], nn)
                    + product(j_buf[part(at), :], t[IJ, cols, :], nt)
                    + product(k_buf[part(at), :], t[KI, :, cols], nn)).astype(BF16)

            wide_loop(body)

        @pl.loop(0, CHUNKS)
        def _(c):
            at = turn(lax.rem(c + early, CHUNKS))

            @pl.when(c < early)
            def _():
                k_copy(at).wait_recv()

                @pl.when(c >= 2)
                def _():
                    res_copy(turn(c + early - 2)).wait_send()

                outer_result(stage_o, lax.rem(at, 2), x, at)
                res_copy(at).start()

            @pl.when(c >= 2)
            def _():
                out_copy(turn(lax.rem(c + early - 2, CHUNKS))).wait()

            inner_result(at)
            out_copy(at).start()

        @pl.loop(CHUNKS - 2, CHUNKS)
        def _(c):
            out_copy(turn(c - early)).wait()
            res_copy(turn(c)).wait_send()

        @pl.loop(0, CHUNKS)
        def _(c):
            j_copy(c).wait_send()
            k_copy(c).wait_send()

        @pl.loop(0, early)
        def _(c):
            for kind in range(3):
                raw_copy(kind, turn(c)).wait_send()


def cycle_of_four(three_index, occupied_energy, virtual_energy):
    rows, _, width = three_index.shape
    half = width // 2
    size = rows // CHUNKS
    flags = pltpu.SemaphoreType.DMA
    scratch = [
        pltpu.VMEM((rows, width), BF16), pltpu.VMEM((rows, width), BF16),
        pltpu.VMEM((rows, width), BF16),
        pltpu.VMEM((2, size, width), BF16), pltpu.VMEM((2, size, width), BF16),
        pltpu.VMEM((4, width, width), F32), pltpu.VMEM((5, width, width), BF16),
        pltpu.VMEM((half, width), BF16), pltpu.VMEM((half, width), BF16),
        pltpu.VMEM((4, half, width), F32),
        pltpu.VMEM((4, half, width), BF16), pltpu.VMEM((4, half, width), BF16),
        pltpu.VMEM((3, 8, 128), F32),
    ]
    scratch += [flags((CHUNKS,))] * 8 + [flags((3, CHUNKS))] * 2 + [flags((3,))] * 2 + [flags] * 2
    scratch += [flags((4,))] * 4 + [flags((5,))] * 4 + [flags] * 2 + [flags((3,))]
    vmem = pl.BlockSpec(memory_space=pltpu.VMEM)
    density = pl.pallas_call(
        four_blocks,
        out_shape=jax.ShapeDtypeStruct((rows, width), BF16),
        in_specs=[vmem] * 4,
        out_specs=pl.BlockSpec(memory_space=pl.ANY),
        scratch_shapes=scratch,
        compiler_params=pltpu.CompilerParams(
            collective_id=0, has_side_effects=True, vmem_limit_bytes=67_000_000),
    )(
        three_index.reshape(rows, width),
        jnp.broadcast_to(occupied_energy.astype(F32)[:, None], (8, 128)),
        virtual_energy[None, :],
        virtual_energy[:, None],
    )
    return density.reshape(rows, 1, width)


def solution(mesh):
    placed = (P("aux", "occ", "virt"), P("occ"), P("virt"))

    def on_device(three_index, occupied_energy, virtual_energy):
        paired = mesh.shape["occ"] == 4 and mesh.shape["aux"] == 4 and three_index.shape[1] == 1
        body = cycle_of_four if paired else any_cycle
        return body(three_index, occupied_energy, virtual_energy)

    return jax.shard_map(
        on_device, mesh=mesh, in_specs=placed, out_specs=P("aux", "occ", "virt"), check_vma=False
    )
```

```python
import functools

import jax
import jax.numpy as jnp
from jax import lax
from jax.experimental import pallas as pl
from jax.experimental.pallas import tpu as pltpu
from jax.sharding import PartitionSpec as P

spin_scale = 1.2
MESH = pl.DeviceIdType.MESH
CHUNKS = 16
WIDE = 256
F32, BF16 = jnp.float32, jnp.bfloat16


def shifted(block, axis, distance):
    devices = range(lax.axis_size(axis))
    route = [((i - distance) % len(devices), i) for i in devices]
    return lax.ppermute(block, axis, route)


def level_matrix(virtual_energy, left_occupied, right_occupied):
    left_levels = (virtual_energy[None, :] - left_occupied.astype(jnp.float32)[:, None]).reshape(-1)
    right_levels = (virtual_energy[None, :] - right_occupied.astype(jnp.float32)[:, None]).reshape(
        -1
    )
    return left_levels[:, None] + right_levels[None, :]


def amplitudes(own_block, far_block, own_energy, far_energy, virtual_energy):
    partial_sums = lax.dot_general(
        own_block, far_block, (((0,), (0,)), ((), ())), preferred_element_type=jnp.float32
    )
    pair_sums = lax.psum(partial_sums, "aux")
    denominator = level_matrix(virtual_energy, own_energy, far_energy)
    return (spin_scale * pair_sums / denominator).astype(jnp.bfloat16)


def any_cycle(three_index, occupied_energy, virtual_energy):
    aux_rows, occ_rows, slab_size = three_index.shape
    own_block = three_index.reshape(aux_rows, occ_rows * slab_size)
    first_index, first_energy = shifted((three_index, occupied_energy), "occ", 1)
    second_index, second_energy = shifted((first_index, first_energy), "occ", 1)
    first_block = first_index.reshape(aux_rows, occ_rows * slab_size)
    second_block = second_index.reshape(aux_rows, occ_rows * slab_size)
    later_one = shifted(own_block, "occ", -1)
    later_two = shifted(own_block, "occ", -2)
    first_amplitude = amplitudes(
        own_block, first_block, occupied_energy, first_energy, virtual_energy
    )
    accumulated = lax.dot_general(
        first_block, first_amplitude, (((1,), (1,)), ((), ())), preferred_element_type=jnp.float32
    )
    arrived_one = shifted(first_amplitude, "occ", -1)
    accumulated = accumulated + jnp.dot(later_one, arrived_one, preferred_element_type=jnp.float32)
    second_amplitude = amplitudes(
        own_block, second_block, occupied_energy, second_energy, virtual_energy
    )
    accumulated = accumulated + lax.dot_general(
        second_block, second_amplitude, (((1,), (1,)), ((), ())), preferred_element_type=jnp.float32
    )
    arrived_two = shifted(second_amplitude, "occ", -2)
    accumulated = accumulated + jnp.dot(later_two, arrived_two, preferred_element_type=jnp.float32)
    return accumulated.astype(jnp.bfloat16).reshape(aux_rows, occ_rows, slab_size)


OI, OJ, IJ, OK, KI = range(5)


def four_blocks(x, e_own, e_row, out, o_buf, j_buf, k_buf, stage_o, stage_i, g, t,
                z_out, z_in, c_in, x_out, x_in, e_col, e_buf,
                o_s, o_r, j_s, j_r, k_s, k_r, res_s, res_r, raw_s, raw_r, e_s, e_r, z_s, z_r,
                c_s, c_r, x_s, x_r, t_s, t_r, go_s, go_r, ki_s, ki_r, out_s):
    rows, width = x.shape
    size, half, early = rows // CHUNKS, width // 2, CHUNKS // 2
    v, z, a = lax.axis_index("virt"), lax.axis_index("occ"), lax.axis_index("aux")
    core = lax.rem(a, 2)
    inner = jnp.logical_or(z == 1, z == 2)
    outer = jnp.logical_or(z == 0, z == 3)
    mate_z = z + 1 - 2 * lax.rem(z, 2)
    mate, mirror = (v, mate_z, a), (v, 3 - z, a)
    core_mate, x_mate = (v, z, a + 1 - 2 * core), (v, z, lax.rem(a + 2, 4))
    around = [(v, lax.rem(z + d, 4), a) for d in (1, 2, 3)]
    base = early * (z // 2)

    barrier = pltpu.get_barrier_semaphore()
    for peer in around + [core_mate, x_mate]:
        pl.semaphore_signal(barrier, inc=1, device_id=peer, device_id_type=MESH)
    pl.semaphore_wait(barrier, 5)

    def remote(src, dst, send, recv, peer):
        return pltpu.make_async_remote_copy(
            src_ref=src, dst_ref=dst, send_sem=send, recv_sem=recv, device_id=peer,
            device_id_type=MESH)

    def turn(c):
        return lax.rem(c + base, CHUNKS)

    def part(at):
        return pl.ds(pl.multiple_of(at * size, size), size)

    def o_copy(at):
        return remote(x.at[part(at)], o_buf.at[part(at)], o_s.at[at], o_r.at[at], mate)

    def j_copy(at):
        return remote(x.at[part(at)], j_buf.at[part(at)], j_s.at[at], j_r.at[at], mirror)

    def k_copy(at):
        return remote(o_buf.at[part(at)], k_buf.at[part(at)], k_s.at[at], k_r.at[at], mirror)

    def raw_copy(kind, at):
        src, dst = ((x, o_buf), (j_buf, j_buf), (k_buf, k_buf))[kind]
        return remote(src.at[part(at)], dst.at[part(at)], raw_s.at[kind, at], raw_r.at[kind, at],
                      mate)

    def res_copy(at):
        return remote(stage_o.at[lax.rem(at, 2)], o_buf.at[part(at)], res_s.at[at], res_r.at[at],
                      mate)

    def out_copy(at, slot):
        return pltpu.make_async_copy(stage_i.at[slot], out.at[part(at)], out_s.at[slot])

    def direct_copy(at):
        return pltpu.make_async_copy(o_buf.at[part(at)], out.at[part(at)], out_s.at[2])

    mine = pl.ds(pl.multiple_of(core * half, half), half)
    other = pl.ds(pl.multiple_of(half - core * half, half), half)

    def t_copy(p):
        return remote(t.at[p, mine], t.at[p, mine], t_s.at[p], t_r.at[p], core_mate)

    def go_copy(p):
        return remote(t.at[p, mine], t.at[p, mine], go_s.at[p], go_r.at[p], mate)

    nt = (((1,), (1,)), ((), ()))
    nn = (((1,), (0,)), ((), ()))
    tn = (((0,), (0,)), ((), ()))

    def product(left, right, dims):
        return lax.dot_general(left, right, dims, preferred_element_type=F32)

    def wide_loop(body):
        @pl.loop(0, width // WIDE)
        def _(n):
            body(pl.ds(pl.multiple_of(n * WIDE, WIDE), WIDE))

    def outer_result(stage, slot, i_block, at):
        def body(cols):
            stage[slot, :, cols] = (
                product(i_block[part(at), :], t[OI, cols, :], nt)
                + product(j_buf[part(at), :], t[OJ, cols, :], nt)
                + product(k_buf[part(at), :], t[OK, cols, :], nt)).astype(BF16)

        wide_loop(body)

    def gram(pair, left, right, at):
        def body(cols):
            g[pair, :, cols] += product(left[part(at), :], right[part(at), cols], tn)

        wide_loop(body)

    def turn_over():
        @pl.when(z >= 2)
        def _():
            t[OK] = t[OK].T

    energies = [remote(e_own, e_buf.at[d], e_s.at[d], e_r.at[d], around[d]) for d in range(3)]
    for copy in energies:
        copy.start()

    @pl.when(outer)
    def _():
        @pl.loop(0, CHUNKS)
        def _(c):
            o_copy(turn(c)).start()

        for p in (OJ, OI, OK):
            go_copy(p).wait_recv()
            t_copy(p).start()
            t_copy(p).wait()
        turn_over()

        @pl.loop(0, early)
        def _(c):
            at = turn(c)
            for kind in range(3):
                raw_copy(kind, at).wait_recv()

            @pl.when(c >= 2)
            def _():
                out_copy(turn(c - 2), lax.rem(at, 2)).wait()

            outer_result(stage_i, lax.rem(at, 2), o_buf, at)
            out_copy(at, lax.rem(at, 2)).start()

        @pl.loop(early, CHUNKS)
        def _(c):
            res_copy(turn(c)).wait_recv()
            direct_copy(turn(c)).start()
            direct_copy(turn(c)).wait()

        @pl.loop(early - 2, early)
        def _(c):
            out_copy(turn(c), lax.rem(c, 2)).wait()

        @pl.loop(0, CHUNKS)
        def _(c):
            o_copy(c).wait_send()

        for copy in energies:
            copy.wait()

    @pl.when(inner)
    def _():
        @pl.loop(0, CHUNKS)
        def _(c):
            j_copy(lax.rem(turn(c) + early, CHUNKS)).start()

        @pl.loop(0, early)
        def _(c):
            raw_copy(0, turn(c)).start()

        g[...] = jnp.zeros_like(g)
        e_col[...] = jnp.broadcast_to(e_row[...], (8, width)).T

        @pl.loop(0, CHUNKS)
        def _(c):
            at = turn(c)
            j_copy(at).wait_recv()

            @pl.when(c < early)
            def _():
                raw_copy(1, at).start()

            o_copy(at).wait_recv()

            @pl.when(c >= early)
            def _():
                k_copy(at).start()

            gram(OI, o_buf, x, at)
            gram(OJ, o_buf, j_buf, at)
            gram(IJ, x, j_buf, at)

        for copy in energies:
            copy.wait()

        def occupied(block):
            return e_buf[lax.rem(z - block + 3, 4)][0:1, 0:1]

        e_i = e_own[0:1, 0:1]
        e_o, e_j, e_k = occupied(mate_z), occupied(3 - z), occupied(3 - mate_z)

        def core_copy(p):
            return remote(g.at[p, other], c_in.at[p], c_s.at[p], c_r.at[p], core_mate)

        def x_copy(p):
            return remote(x_out.at[p], x_in.at[p], x_s.at[p], x_r.at[p], x_mate)

        def finish(p, left, right, weight):
            x_copy(p).wait()
            sums = g[p, mine, :] + x_in[p].astype(F32)
            levels = (e_col[mine, 0:1] - left) + (e_row[...] - right)
            t[p, mine, :] = ((spin_scale * sums / levels).astype(BF16).astype(F32)
                             * weight).astype(BF16)
            t_copy(p).start()

        for p in (OJ, OI, IJ):
            core_copy(p).start()
        for p in (OJ, OI, IJ):
            core_copy(p).wait()
            g[p, mine, :] += c_in[p]
            x_out[p] = g[p, mine, :].astype(BF16)
            x_copy(p).start()

        def far_pair(c):
            at = turn(c)
            k_copy(at).wait_recv()
            raw_copy(2, at).start()

            @pl.when(z == 1)
            def _():
                gram(OK, o_buf, k_buf, at)

            @pl.when(z == 2)
            def _():
                gram(OK, k_buf, o_buf, at)

        @pl.loop(0, early - 2)
        def _(c):
            far_pair(c)

        ki_copy = remote(t.at[OJ, mine], t.at[KI, mine], ki_s, ki_r, mirror)
        finish(OJ, e_o, e_j, 2.0)
        go_copy(OJ).start()
        ki_copy.start()
        finish(OI, e_o, e_i, 1.0)
        go_copy(OI).start()
        far_pair(early - 2)
        finish(IJ, e_i, e_j, 1.0)
        k_copy(turn(0)).start()
        far_pair(early - 1)

        core_copy(OK).start()
        core_copy(OK).wait()
        g[OK, mine, :] += c_in[OK]
        z_out[...] = g[OK, mine, :].astype(BF16)
        z_copy = remote(z_out, z_in, z_s, z_r, mirror)
        z_copy.start()

        @pl.loop(1, early)
        def _(c):
            k_copy(turn(c)).start()

        z_copy.wait()
        g[OK, mine, :] += z_in[...].astype(F32)
        x_out[OK] = g[OK, mine, :].astype(BF16)
        x_copy(OK).start()
        ki_copy.wait()
        t_copy(KI).start()
        finish(OK, jnp.where(z == 1, e_o, e_k), jnp.where(z == 1, e_k, e_o), 1.0)
        go_copy(OK).start()
        for p in (OJ, OI, IJ, KI, OK):
            t_copy(p).wait()
        for p in (OJ, OI, OK):
            go_copy(p).wait_send()
        turn_over()

        def inner_result(at, slot):
            def body(cols):
                stage_i[slot, :, cols] = (
                    product(o_buf[part(at), :], t[OI, :, cols], nn)
                    + product(j_buf[part(at), :], t[IJ, cols, :], nt)
                    + product(k_buf[part(at), :], t[KI, :, cols], nn)).astype(BF16)

            wide_loop(body)

        @pl.loop(0, early)
        def _(c):
            late = turn(c + early)
            k_copy(late).wait_recv()

            @pl.when(c >= 2)
            def _():
                res_copy(turn(c + early - 2)).wait_send()

            outer_result(stage_o, lax.rem(late, 2), x, late)
            res_copy(late).start()
            for slot, start in ((0, early), (1, 0)):
                at = turn(c + start)

                @pl.when(c >= 1)
                def _():
                    out_copy(turn(c + start - 1), slot).wait()

                inner_result(at, slot)
                out_copy(at, slot).start()

        out_copy(turn(CHUNKS - 1), 0).wait()
        out_copy(turn(early - 1), 1).wait()

        @pl.loop(CHUNKS - 2, CHUNKS)
        def _(c):
            res_copy(turn(c)).wait_send()

        @pl.loop(0, CHUNKS)
        def _(c):
            j_copy(c).wait_send()
            k_copy(c).wait_send()

        @pl.loop(0, early)
        def _(c):
            for kind in range(3):
                raw_copy(kind, turn(c)).wait_send()


def cycle_of_four(three_index, occupied_energy, virtual_energy):
    rows, _, width = three_index.shape
    half = width // 2
    size = rows // CHUNKS
    flags = pltpu.SemaphoreType.DMA
    scratch = [
        pltpu.VMEM((rows, width), BF16), pltpu.VMEM((rows, width), BF16),
        pltpu.VMEM((rows, width), BF16),
        pltpu.VMEM((2, size, width), BF16), pltpu.VMEM((2, size, width), BF16),
        pltpu.VMEM((4, width, width), F32), pltpu.VMEM((5, width, width), BF16),
        pltpu.VMEM((half, width), BF16), pltpu.VMEM((half, width), BF16),
        pltpu.VMEM((4, half, width), F32),
        pltpu.VMEM((4, half, width), BF16), pltpu.VMEM((4, half, width), BF16),
        pltpu.VMEM((width, 8), F32), pltpu.VMEM((3, 8, 128), F32),
    ]
    scratch += [flags((CHUNKS,))] * 8 + [flags((3, CHUNKS))] * 2 + [flags((3,))] * 2 + [flags] * 2
    scratch += [flags((4,))] * 4 + [flags((5,))] * 4 + [flags] * 2 + [flags((3,))]
    vmem = pl.BlockSpec(memory_space=pltpu.VMEM)
    density = pl.pallas_call(
        four_blocks,
        out_shape=jax.ShapeDtypeStruct((rows, width), BF16),
        in_specs=[vmem] * 3,
        out_specs=pl.BlockSpec(memory_space=pl.ANY),
        scratch_shapes=scratch,
        compiler_params=pltpu.CompilerParams(
            collective_id=0, has_side_effects=True, vmem_limit_bytes=67_000_000),
    )(
        three_index.reshape(rows, width),
        jnp.broadcast_to(occupied_energy.astype(F32)[:, None], (8, 128)),
        virtual_energy.reshape(1, width),
    )
    return density.reshape(rows, 1, width)


def solution(mesh):
    placed = (P("aux", "occ", "virt"), P("occ"), P("virt"))

    def on_device(three_index, occupied_energy, virtual_energy):
        paired = mesh.shape["occ"] == 4 and mesh.shape["aux"] == 4 and three_index.shape[1] == 1
        body = cycle_of_four if paired else any_cycle
        return body(three_index, occupied_energy, virtual_energy)

    return jax.shard_map(
        on_device, mesh=mesh, in_specs=placed, out_specs=P("aux", "occ", "virt"), check_vma=False
    )
```

```python
import functools

import jax
import jax.numpy as jnp
from jax import lax
from jax.experimental import pallas as pl
from jax.experimental.pallas import tpu as pltpu
from jax.sharding import PartitionSpec as P

spin_scale = 1.2
MESH = pl.DeviceIdType.MESH
CHUNKS = 8
WIDE = 256
F32, BF16 = jnp.float32, jnp.bfloat16


def shifted(block, axis, distance):
    devices = range(lax.axis_size(axis))
    route = [((i - distance) % len(devices), i) for i in devices]
    return lax.ppermute(block, axis, route)


def level_matrix(virtual_energy, left_occupied, right_occupied):
    left_levels = (virtual_energy[None, :] - left_occupied.astype(jnp.float32)[:, None]).reshape(-1)
    right_levels = (virtual_energy[None, :] - right_occupied.astype(jnp.float32)[:, None]).reshape(
        -1
    )
    return left_levels[:, None] + right_levels[None, :]


def amplitudes(own_block, far_block, own_energy, far_energy, virtual_energy):
    partial_sums = lax.dot_general(
        own_block, far_block, (((0,), (0,)), ((), ())), preferred_element_type=jnp.float32
    )
    pair_sums = lax.psum(partial_sums, "aux")
    denominator = level_matrix(virtual_energy, own_energy, far_energy)
    return (spin_scale * pair_sums / denominator).astype(jnp.bfloat16)


def any_cycle(three_index, occupied_energy, virtual_energy):
    aux_rows, occ_rows, slab_size = three_index.shape
    own_block = three_index.reshape(aux_rows, occ_rows * slab_size)
    first_index, first_energy = shifted((three_index, occupied_energy), "occ", 1)
    second_index, second_energy = shifted((first_index, first_energy), "occ", 1)
    first_block = first_index.reshape(aux_rows, occ_rows * slab_size)
    second_block = second_index.reshape(aux_rows, occ_rows * slab_size)
    later_one = shifted(own_block, "occ", -1)
    later_two = shifted(own_block, "occ", -2)
    first_amplitude = amplitudes(
        own_block, first_block, occupied_energy, first_energy, virtual_energy
    )
    accumulated = lax.dot_general(
        first_block, first_amplitude, (((1,), (1,)), ((), ())), preferred_element_type=jnp.float32
    )
    arrived_one = shifted(first_amplitude, "occ", -1)
    accumulated = accumulated + jnp.dot(later_one, arrived_one, preferred_element_type=jnp.float32)
    second_amplitude = amplitudes(
        own_block, second_block, occupied_energy, second_energy, virtual_energy
    )
    accumulated = accumulated + lax.dot_general(
        second_block, second_amplitude, (((1,), (1,)), ((), ())), preferred_element_type=jnp.float32
    )
    arrived_two = shifted(second_amplitude, "occ", -2)
    accumulated = accumulated + jnp.dot(later_two, arrived_two, preferred_element_type=jnp.float32)
    return accumulated.astype(jnp.bfloat16).reshape(aux_rows, occ_rows, slab_size)


OI, OJ, IJ, OK, KI, FAR = range(6)


def four_blocks(x, e_own, e_row, out, o_buf, j_buf, k_buf, stage_o, stage_i, g, t,
                z_out, z_in, c_in, x_out, x_in, e_col, e_buf,
                o_s, o_r, j_s, j_r, k_s, k_r, res_s, res_r, raw_s, raw_r, e_s, e_r, z_s, z_r,
                c_s, c_r, x_s, x_r, t_s, t_r, go_s, go_r, ki_s, ki_r, out_s):
    rows, width = x.shape
    size, half, early = rows // CHUNKS, width // 2, CHUNKS // 2
    v, z, a = lax.axis_index("virt"), lax.axis_index("occ"), lax.axis_index("aux")
    core = lax.rem(a, 2)
    inner = jnp.logical_or(z == 1, z == 2)
    outer = jnp.logical_or(z == 0, z == 3)
    mate_z = z + 1 - 2 * lax.rem(z, 2)
    mate, mirror = (v, mate_z, a), (v, 3 - z, a)
    core_mate, x_mate = (v, z, a + 1 - 2 * core), (v, z, lax.rem(a + 2, 4))
    around = [(v, lax.rem(z + d, 4), a) for d in (1, 2, 3)]
    base = early * (z // 2)

    barrier = pltpu.get_barrier_semaphore()
    for peer in around + [core_mate, x_mate]:
        pl.semaphore_signal(barrier, inc=1, device_id=peer, device_id_type=MESH)
    pl.semaphore_wait(barrier, 5)

    def remote(src, dst, send, recv, peer):
        return pltpu.make_async_remote_copy(
            src_ref=src, dst_ref=dst, send_sem=send, recv_sem=recv, device_id=peer,
            device_id_type=MESH)

    def turn(c):
        return lax.rem(c + base, CHUNKS)

    def part(at):
        return pl.ds(pl.multiple_of(at * size, size), size)

    def o_copy(at):
        return remote(x.at[part(at)], o_buf.at[part(at)], o_s.at[at], o_r.at[at], mate)

    def j_copy(at):
        return remote(x.at[part(at)], j_buf.at[part(at)], j_s.at[at], j_r.at[at], mirror)

    def k_copy(at):
        return remote(o_buf.at[part(at)], k_buf.at[part(at)], k_s.at[at], k_r.at[at], mirror)

    def raw_copy(kind, at):
        src, dst = ((x, o_buf), (j_buf, j_buf), (k_buf, k_buf))[kind]
        return remote(src.at[part(at)], dst.at[part(at)], raw_s.at[kind, at], raw_r.at[kind, at],
                      mate)

    def res_copy(at):
        return remote(stage_o.at[lax.rem(at, 2)], o_buf.at[part(at)], res_s.at[at], res_r.at[at],
                      mate)

    def out_copy(at, slot):
        return pltpu.make_async_copy(stage_i.at[slot], out.at[part(at)], out_s.at[slot])

    def direct_copy(at):
        return pltpu.make_async_copy(o_buf.at[part(at)], out.at[part(at)], out_s.at[2])

    mine = pl.ds(pl.multiple_of(core * half, half), half)
    other = pl.ds(pl.multiple_of(half - core * half, half), half)

    def t_copy(p):
        return remote(t.at[p, mine], t.at[p, mine], t_s.at[p], t_r.at[p], core_mate)

    def go_copy(p):
        return remote(t.at[p, mine], t.at[p, mine], go_s.at[p], go_r.at[p], mate)

    nt = (((1,), (1,)), ((), ()))
    nn = (((1,), (0,)), ((), ()))
    tn = (((0,), (0,)), ((), ()))

    def product(left, right, dims):
        return lax.dot_general(left, right, dims, preferred_element_type=F32)

    def wide_loop(body):
        @pl.loop(0, width // WIDE)
        def _(n):
            body(pl.ds(pl.multiple_of(n * WIDE, WIDE), WIDE))

    def outer_result(stage, slot, i_block, at):
        def body(cols):
            stage[slot, :, cols] = (
                product(i_block[part(at), :], t[OI, cols, :], nt)
                + product(j_buf[part(at), :], t[OJ, cols, :], nt)
                + product(k_buf[part(at), :], t[FAR, cols, :], nt)).astype(BF16)

        wide_loop(body)

    def gram(pair, left, right, at):
        def body(cols):
            g[pair, :, cols] += product(left[part(at), :], right[part(at), cols], tn)

        wide_loop(body)

    def turn_over():
        @pl.when(z < 2)
        def _():
            t[FAR] = t[OK]

        @pl.when(z >= 2)
        def _():
            t[FAR] = t[OK].T

    energies = [remote(e_own, e_buf.at[d], e_s.at[d], e_r.at[d], around[d]) for d in range(3)]
    for copy in energies:
        copy.start()

    @pl.when(outer)
    def _():
        @pl.loop(0, CHUNKS)
        def _(c):
            o_copy(turn(c)).start()

        for p in (OJ, OI, OK):
            go_copy(p).wait_recv()
            t_copy(p).start()
            t_copy(p).wait()
        turn_over()

        @pl.loop(0, early)
        def _(c):
            at = turn(c)
            for kind in range(3):
                raw_copy(kind, at).wait_recv()

            @pl.when(c >= 2)
            def _():
                out_copy(turn(c - 2), lax.rem(at, 2)).wait()

            outer_result(stage_i, lax.rem(at, 2), o_buf, at)
            out_copy(at, lax.rem(at, 2)).start()

        @pl.loop(early, CHUNKS)
        def _(c):
            res_copy(turn(c)).wait_recv()
            direct_copy(turn(c)).start()
            direct_copy(turn(c)).wait()

        @pl.loop(early - 2, early)
        def _(c):
            out_copy(turn(c), lax.rem(c, 2)).wait()

        @pl.loop(0, CHUNKS)
        def _(c):
            o_copy(c).wait_send()

        for copy in energies:
            copy.wait()

    @pl.when(inner)
    def _():
        @pl.loop(0, CHUNKS)
        def _(c):
            j_copy(lax.rem(turn(c) + early, CHUNKS)).start()

        @pl.loop(0, early)
        def _(c):
            raw_copy(0, turn(c)).start()

        g[...] = jnp.zeros_like(g)
        e_col[...] = jnp.broadcast_to(e_row[...], (8, width)).T

        @pl.loop(0, CHUNKS)
        def _(c):
            at = turn(c)
            j_copy(at).wait_recv()

            @pl.when(c < early)
            def _():
                raw_copy(1, at).start()

            o_copy(at).wait_recv()

            @pl.when(c >= early)
            def _():
                k_copy(at).start()

            gram(OI, o_buf, x, at)
            gram(OJ, o_buf, j_buf, at)
            gram(IJ, x, j_buf, at)

        for copy in energies:
            copy.wait()

        def occupied(block):
            return e_buf[lax.rem(z - block + 3, 4)][0:1, 0:1]

        e_i = e_own[0:1, 0:1]
        e_o, e_j, e_k = occupied(mate_z), occupied(3 - z), occupied(3 - mate_z)

        def core_copy(p):
            return remote(g.at[p, other], c_in.at[p], c_s.at[p], c_r.at[p], core_mate)

        def x_copy(p):
            return remote(x_out.at[p], x_in.at[p], x_s.at[p], x_r.at[p], x_mate)

        def finish(p, left, right, weight):
            x_copy(p).wait()
            sums = g[p, mine, :] + x_in[p].astype(F32)
            levels = (e_col[mine, 0:1] - left) + (e_row[...] - right)
            t[p, mine, :] = ((spin_scale * sums / levels).astype(BF16).astype(F32)
                             * weight).astype(BF16)
            t_copy(p).start()

        for p in (OJ, OI, IJ):
            core_copy(p).start()
        for p in (OJ, OI, IJ):
            core_copy(p).wait()
            g[p, mine, :] += c_in[p]
            x_out[p] = g[p, mine, :].astype(BF16)
            x_copy(p).start()

        def far_pair(c):
            at = turn(c)
            k_copy(at).wait_recv()
            raw_copy(2, at).start()

            @pl.when(z == 1)
            def _():
                gram(OK, o_buf, k_buf, at)

            @pl.when(z == 2)
            def _():
                gram(OK, k_buf, o_buf, at)

        @pl.loop(0, early - 2)
        def _(c):
            far_pair(c)

        ki_copy = remote(t.at[OJ, mine], t.at[KI, mine], ki_s, ki_r, mirror)
        finish(OJ, e_o, e_j, 2.0)
        go_copy(OJ).start()
        ki_copy.start()
        finish(OI, e_o, e_i, 1.0)
        go_copy(OI).start()
        far_pair(early - 2)
        finish(IJ, e_i, e_j, 1.0)
        far_pair(early - 1)

        core_copy(OK).start()
        core_copy(OK).wait()
        g[OK, mine, :] += c_in[OK]
        z_out[...] = g[OK, mine, :].astype(BF16)
        z_copy = remote(z_out, z_in, z_s, z_r, mirror)
        z_copy.start()

        @pl.loop(0, early)
        def _(c):
            k_copy(turn(c)).start()

        z_copy.wait()
        g[OK, mine, :] += z_in[...].astype(F32)
        x_out[OK] = g[OK, mine, :].astype(BF16)
        x_copy(OK).start()
        ki_copy.wait()
        t_copy(KI).start()
        for p in (OJ, OI, IJ, KI):
            t_copy(p).wait()

        def inner_result(c):
            at, slot = turn(c), lax.rem(c, 2)

            @pl.when(c >= 2)
            def _():
                out_copy(turn(c - 2), slot).wait()

            def body(cols):
                stage_i[slot, :, cols] = (
                    product(o_buf[part(at), :], t[OI, :, cols], nn)
                    + product(j_buf[part(at), :], t[IJ, cols, :], nt)
                    + product(k_buf[part(at), :], t[KI, :, cols], nn)).astype(BF16)

            wide_loop(body)
            out_copy(at, slot).start()

        @pl.loop(0, early)
        def _(c):
            inner_result(c)

        finish(OK, jnp.where(z == 1, e_o, e_k), jnp.where(z == 1, e_k, e_o), 1.0)
        go_copy(OK).start()
        t_copy(OK).wait()
        turn_over()

        @pl.loop(early, CHUNKS)
        def _(c):
            at = turn(c)
            k_copy(at).wait_recv()

            @pl.when(c >= early + 2)
            def _():
                res_copy(turn(c - 2)).wait_send()

            outer_result(stage_o, lax.rem(at, 2), x, at)
            res_copy(at).start()
            inner_result(c)

        for p in (OJ, OI, OK):
            go_copy(p).wait_send()

        @pl.loop(CHUNKS - 2, CHUNKS)
        def _(c):
            out_copy(turn(c), lax.rem(c, 2)).wait()

        @pl.loop(CHUNKS - 2, CHUNKS)
        def _(c):
            res_copy(turn(c)).wait_send()

        @pl.loop(0, CHUNKS)
        def _(c):
            j_copy(c).wait_send()
            k_copy(c).wait_send()

        @pl.loop(0, early)
        def _(c):
            for kind in range(3):
                raw_copy(kind, turn(c)).wait_send()


def cycle_of_four(three_index, occupied_energy, virtual_energy):
    rows, _, width = three_index.shape
    half = width // 2
    size = rows // CHUNKS
    flags = pltpu.SemaphoreType.DMA
    scratch = [
        pltpu.VMEM((rows, width), BF16), pltpu.VMEM((rows, width), BF16),
        pltpu.VMEM((rows, width), BF16),
        pltpu.VMEM((2, size, width), BF16), pltpu.VMEM((2, size, width), BF16),
        pltpu.VMEM((4, width, width), F32), pltpu.VMEM((6, width, width), BF16),
        pltpu.VMEM((half, width), BF16), pltpu.VMEM((half, width), BF16),
        pltpu.VMEM((4, half, width), F32),
        pltpu.VMEM((4, half, width), BF16), pltpu.VMEM((4, half, width), BF16),
        pltpu.VMEM((width, 8), F32), pltpu.VMEM((3, 8, 128), F32),
    ]
    scratch += [flags((CHUNKS,))] * 8 + [flags((3, CHUNKS))] * 2 + [flags((3,))] * 2 + [flags] * 2
    scratch += [flags((4,))] * 4 + [flags((5,))] * 4 + [flags] * 2 + [flags((3,))]
    vmem = pl.BlockSpec(memory_space=pltpu.VMEM)
    density = pl.pallas_call(
        four_blocks,
        out_shape=jax.ShapeDtypeStruct((rows, width), BF16),
        in_specs=[vmem] * 3,
        out_specs=pl.BlockSpec(memory_space=pl.ANY),
        scratch_shapes=scratch,
        compiler_params=pltpu.CompilerParams(
            collective_id=0, has_side_effects=True, vmem_limit_bytes=67_000_000),
    )(
        three_index.reshape(rows, width),
        jnp.broadcast_to(occupied_energy.astype(F32)[:, None], (8, 128)),
        virtual_energy.reshape(1, width),
    )
    return density.reshape(rows, 1, width)


def solution(mesh):
    placed = (P("aux", "occ", "virt"), P("occ"), P("virt"))

    def on_device(three_index, occupied_energy, virtual_energy):
        paired = mesh.shape["occ"] == 4 and mesh.shape["aux"] == 4 and three_index.shape[1] == 1
        body = cycle_of_four if paired else any_cycle
        return body(three_index, occupied_energy, virtual_energy)

    return jax.shard_map(
        on_device, mesh=mesh, in_specs=placed, out_specs=P("aux", "occ", "virt"), check_vma=False
    )
```

```python
import functools

import jax
import jax.numpy as jnp
from jax import lax
from jax.experimental import pallas as pl
from jax.experimental.pallas import tpu as pltpu
from jax.sharding import PartitionSpec as P

spin_scale = 1.2
MESH = pl.DeviceIdType.MESH
CHUNKS = 8
WIDE = 256
F32, BF16 = jnp.float32, jnp.bfloat16


def shifted(block, axis, distance):
    devices = range(lax.axis_size(axis))
    route = [((i - distance) % len(devices), i) for i in devices]
    return lax.ppermute(block, axis, route)


def level_matrix(virtual_energy, left_occupied, right_occupied):
    left_levels = (virtual_energy[None, :] - left_occupied.astype(jnp.float32)[:, None]).reshape(-1)
    right_levels = (virtual_energy[None, :] - right_occupied.astype(jnp.float32)[:, None]).reshape(
        -1
    )
    return left_levels[:, None] + right_levels[None, :]


def amplitudes(own_block, far_block, own_energy, far_energy, virtual_energy):
    partial_sums = lax.dot_general(
        own_block, far_block, (((0,), (0,)), ((), ())), preferred_element_type=jnp.float32
    )
    pair_sums = lax.psum(partial_sums, "aux")
    denominator = level_matrix(virtual_energy, own_energy, far_energy)
    return (spin_scale * pair_sums / denominator).astype(jnp.bfloat16)


def any_cycle(three_index, occupied_energy, virtual_energy):
    aux_rows, occ_rows, slab_size = three_index.shape
    own_block = three_index.reshape(aux_rows, occ_rows * slab_size)
    first_index, first_energy = shifted((three_index, occupied_energy), "occ", 1)
    second_index, second_energy = shifted((first_index, first_energy), "occ", 1)
    first_block = first_index.reshape(aux_rows, occ_rows * slab_size)
    second_block = second_index.reshape(aux_rows, occ_rows * slab_size)
    later_one = shifted(own_block, "occ", -1)
    later_two = shifted(own_block, "occ", -2)
    first_amplitude = amplitudes(
        own_block, first_block, occupied_energy, first_energy, virtual_energy
    )
    accumulated = lax.dot_general(
        first_block, first_amplitude, (((1,), (1,)), ((), ())), preferred_element_type=jnp.float32
    )
    arrived_one = shifted(first_amplitude, "occ", -1)
    accumulated = accumulated + jnp.dot(later_one, arrived_one, preferred_element_type=jnp.float32)
    second_amplitude = amplitudes(
        own_block, second_block, occupied_energy, second_energy, virtual_energy
    )
    accumulated = accumulated + lax.dot_general(
        second_block, second_amplitude, (((1,), (1,)), ((), ())), preferred_element_type=jnp.float32
    )
    arrived_two = shifted(second_amplitude, "occ", -2)
    accumulated = accumulated + jnp.dot(later_two, arrived_two, preferred_element_type=jnp.float32)
    return accumulated.astype(jnp.bfloat16).reshape(aux_rows, occ_rows, slab_size)


OI, OJ, IJ, OK, KI, FAR = range(6)


def four_blocks(x, e_own, e_row, out, o_buf, j_buf, k_buf, stage_o, stage_i, g, t,
                z_out, z_in, c_in, x_out, x_in, e_col, e_buf,
                o_s, o_r, j_s, j_r, k_s, k_r, res_s, res_r, raw_s, raw_r, e_s, e_r, z_s, z_r,
                c_s, c_r, x_s, x_r, t_s, t_r, go_s, go_r, ki_s, ki_r, out_s):
    rows, width = x.shape
    size, half, early = rows // CHUNKS, width // 2, CHUNKS // 2
    v, z, a = lax.axis_index("virt"), lax.axis_index("occ"), lax.axis_index("aux")
    core = lax.rem(a, 2)
    inner = jnp.logical_or(z == 1, z == 2)
    outer = jnp.logical_or(z == 0, z == 3)
    mate_z = z + 1 - 2 * lax.rem(z, 2)
    mate, mirror = (v, mate_z, a), (v, 3 - z, a)
    core_mate, x_mate = (v, z, a + 1 - 2 * core), (v, z, lax.rem(a + 2, 4))
    around = [(v, lax.rem(z + d, 4), a) for d in (1, 2, 3)]
    base = early * (z // 2)

    barrier = pltpu.get_barrier_semaphore()
    for peer in around + [core_mate, x_mate]:
        pl.semaphore_signal(barrier, inc=1, device_id=peer, device_id_type=MESH)
    pl.semaphore_wait(barrier, 5)

    def remote(src, dst, send, recv, peer):
        return pltpu.make_async_remote_copy(
            src_ref=src, dst_ref=dst, send_sem=send, recv_sem=recv, device_id=peer,
            device_id_type=MESH)

    def turn(c):
        return lax.rem(c + base, CHUNKS)

    def part(at):
        return pl.ds(pl.multiple_of(at * size, size), size)

    def o_copy(at):
        return remote(x.at[part(at)], o_buf.at[part(at)], o_s.at[at], o_r.at[at], mate)

    def j_copy(at):
        return remote(x.at[part(at)], j_buf.at[part(at)], j_s.at[at], j_r.at[at], mirror)

    def k_copy(at):
        return remote(o_buf.at[part(at)], k_buf.at[part(at)], k_s.at[at], k_r.at[at], mirror)

    def raw_copy(kind, at):
        src, dst = ((x, o_buf), (j_buf, j_buf), (k_buf, k_buf))[kind]
        return remote(src.at[part(at)], dst.at[part(at)], raw_s.at[kind, at], raw_r.at[kind, at],
                      mate)

    def res_copy(at):
        return remote(stage_o.at[lax.rem(at, 2)], o_buf.at[part(at)], res_s.at[at], res_r.at[at],
                      mate)

    def out_copy(at, slot):
        return pltpu.make_async_copy(stage_i.at[slot], out.at[part(at)], out_s.at[slot])

    def direct_copy(at):
        return pltpu.make_async_copy(o_buf.at[part(at)], out.at[part(at)], out_s.at[2])

    mine = pl.ds(pl.multiple_of(core * half, half), half)
    other = pl.ds(pl.multiple_of(half - core * half, half), half)

    def t_copy(p):
        return remote(t.at[p, mine], t.at[p, mine], t_s.at[p], t_r.at[p], core_mate)

    def go_copy(p):
        return remote(t.at[p, mine], t.at[p, mine], go_s.at[p], go_r.at[p], mate)

    nt = (((1,), (1,)), ((), ()))
    nn = (((1,), (0,)), ((), ()))
    tn = (((0,), (0,)), ((), ()))

    def product(left, right, dims):
        return lax.dot_general(left, right, dims, preferred_element_type=F32)

    def wide_loop(body):
        @pl.loop(0, width // WIDE)
        def _(n):
            body(pl.ds(pl.multiple_of(n * WIDE, WIDE), WIDE))

    def outer_result(stage, slot, i_block, at):
        def body(cols):
            stage[slot, :, cols] = (
                product(i_block[part(at), :], t[OI, cols, :], nt)
                + product(j_buf[part(at), :], t[OJ, cols, :], nt)
                + product(k_buf[part(at), :], t[FAR, cols, :], nt)).astype(BF16)

        wide_loop(body)

    def gram(pair, left, right, at):
        g[pair] += product(left[part(at), :], right[part(at), :], tn)

    def turn_over():
        @pl.when(z < 2)
        def _():
            t[FAR] = t[OK]

        @pl.when(z >= 2)
        def _():
            t[FAR] = t[OK].T

    energies = [remote(e_own, e_buf.at[d], e_s.at[d], e_r.at[d], around[d]) for d in range(3)]
    for copy in energies:
        copy.start()

    @pl.when(outer)
    def _():
        @pl.loop(0, CHUNKS)
        def _(c):
            o_copy(turn(c)).start()

        for p in (OJ, OI, OK):
            go_copy(p).wait_recv()
            t_copy(p).start()
            t_copy(p).wait()
        turn_over()

        @pl.loop(0, early)
        def _(c):
            at = turn(c)
            for kind in range(3):
                raw_copy(kind, at).wait_recv()

            @pl.when(c >= 2)
            def _():
                out_copy(turn(c - 2), lax.rem(at, 2)).wait()

            outer_result(stage_i, lax.rem(at, 2), o_buf, at)
            out_copy(at, lax.rem(at, 2)).start()

        @pl.loop(early, CHUNKS)
        def _(c):
            res_copy(turn(c)).wait_recv()
            direct_copy(turn(c)).start()
            direct_copy(turn(c)).wait()

        @pl.loop(early - 2, early)
        def _(c):
            out_copy(turn(c), lax.rem(c, 2)).wait()

        @pl.loop(0, CHUNKS)
        def _(c):
            o_copy(c).wait_send()

        for copy in energies:
            copy.wait()

    @pl.when(inner)
    def _():
        @pl.loop(0, CHUNKS)
        def _(c):
            j_copy(lax.rem(turn(c) + early, CHUNKS)).start()

        @pl.loop(0, early)
        def _(c):
            raw_copy(0, turn(c)).start()

        g[...] = jnp.zeros_like(g)
        e_col[...] = jnp.broadcast_to(e_row[...], (8, width)).T

        @pl.loop(0, CHUNKS)
        def _(c):
            at = turn(c)
            j_copy(at).wait_recv()

            @pl.when(c < early)
            def _():
                raw_copy(1, at).start()

            o_copy(at).wait_recv()

            @pl.when(c >= early)
            def _():
                k_copy(at).start()

            gram(OI, o_buf, x, at)
            gram(OJ, o_buf, j_buf, at)
            gram(IJ, x, j_buf, at)

        for copy in energies:
            copy.wait()

        def occupied(block):
            return e_buf[lax.rem(z - block + 3, 4)][0:1, 0:1]

        e_i = e_own[0:1, 0:1]
        e_o, e_j, e_k = occupied(mate_z), occupied(3 - z), occupied(3 - mate_z)

        def core_copy(p):
            return remote(g.at[p, other], c_in.at[p], c_s.at[p], c_r.at[p], core_mate)

        def x_copy(p):
            return remote(x_out.at[p], x_in.at[p], x_s.at[p], x_r.at[p], x_mate)

        def finish(p, left, right, weight):
            x_copy(p).wait()
            sums = g[p, mine, :] + x_in[p].astype(F32)
            levels = (e_col[mine, 0:1] - left) + (e_row[...] - right)
            t[p, mine, :] = ((spin_scale * sums / levels).astype(BF16).astype(F32)
                             * weight).astype(BF16)
            t_copy(p).start()

        for p in (OJ, OI, IJ):
            core_copy(p).start()
        for p in (OJ, OI, IJ):
            core_copy(p).wait()
            g[p, mine, :] += c_in[p]
            x_out[p] = g[p, mine, :].astype(BF16)
            x_copy(p).start()

        def far_pair(c):
            at = turn(c)
            k_copy(at).wait_recv()
            raw_copy(2, at).start()

            @pl.when(z == 1)
            def _():
                gram(OK, o_buf, k_buf, at)

            @pl.when(z == 2)
            def _():
                gram(OK, k_buf, o_buf, at)

        @pl.loop(0, early - 2)
        def _(c):
            far_pair(c)

        ki_copy = remote(t.at[OJ, mine], t.at[KI, mine], ki_s, ki_r, mirror)
        finish(OJ, e_o, e_j, 2.0)
        go_copy(OJ).start()
        ki_copy.start()
        finish(OI, e_o, e_i, 1.0)
        go_copy(OI).start()
        far_pair(early - 2)
        finish(IJ, e_i, e_j, 1.0)
        far_pair(early - 1)

        core_copy(OK).start()
        core_copy(OK).wait()
        g[OK, mine, :] += c_in[OK]
        z_out[...] = g[OK, mine, :].astype(BF16)
        z_copy = remote(z_out, z_in, z_s, z_r, mirror)
        z_copy.start()

        @pl.loop(0, early)
        def _(c):
            k_copy(turn(c)).start()

        z_copy.wait()
        g[OK, mine, :] += z_in[...].astype(F32)
        x_out[OK] = g[OK, mine, :].astype(BF16)
        x_copy(OK).start()
        ki_copy.wait()
        t_copy(KI).start()
        for p in (OJ, OI, IJ, KI):
            t_copy(p).wait()

        def inner_result(c):
            at, slot = turn(c), lax.rem(c, 2)

            @pl.when(c >= 2)
            def _():
                out_copy(turn(c - 2), slot).wait()

            def body(cols):
                stage_i[slot, :, cols] = (
                    product(o_buf[part(at), :], t[OI, :, cols], nn)
                    + product(j_buf[part(at), :], t[IJ, cols, :], nt)
                    + product(k_buf[part(at), :], t[KI, :, cols], nn)).astype(BF16)

            wide_loop(body)
            out_copy(at, slot).start()

        @pl.loop(0, early)
        def _(c):
            inner_result(c)

        finish(OK, jnp.where(z == 1, e_o, e_k), jnp.where(z == 1, e_k, e_o), 1.0)
        go_copy(OK).start()
        t_copy(OK).wait()
        turn_over()

        @pl.loop(early, CHUNKS)
        def _(c):
            at = turn(c)
            k_copy(at).wait_recv()

            @pl.when(c >= early + 2)
            def _():
                res_copy(turn(c - 2)).wait_send()

            outer_result(stage_o, lax.rem(at, 2), x, at)
            res_copy(at).start()
            inner_result(c)

        for p in (OJ, OI, OK):
            go_copy(p).wait_send()

        @pl.loop(CHUNKS - 2, CHUNKS)
        def _(c):
            out_copy(turn(c), lax.rem(c, 2)).wait()

        @pl.loop(CHUNKS - 2, CHUNKS)
        def _(c):
            res_copy(turn(c)).wait_send()

        @pl.loop(0, CHUNKS)
        def _(c):
            j_copy(c).wait_send()
            k_copy(c).wait_send()

        @pl.loop(0, early)
        def _(c):
            for kind in range(3):
                raw_copy(kind, turn(c)).wait_send()


def cycle_of_four(three_index, occupied_energy, virtual_energy):
    rows, _, width = three_index.shape
    half = width // 2
    size = rows // CHUNKS
    flags = pltpu.SemaphoreType.DMA
    scratch = [
        pltpu.VMEM((rows, width), BF16), pltpu.VMEM((rows, width), BF16),
        pltpu.VMEM((rows, width), BF16),
        pltpu.VMEM((2, size, width), BF16), pltpu.VMEM((2, size, width), BF16),
        pltpu.VMEM((4, width, width), F32), pltpu.VMEM((6, width, width), BF16),
        pltpu.VMEM((half, width), BF16), pltpu.VMEM((half, width), BF16),
        pltpu.VMEM((4, half, width), F32),
        pltpu.VMEM((4, half, width), BF16), pltpu.VMEM((4, half, width), BF16),
        pltpu.VMEM((width, 8), F32), pltpu.VMEM((3, 8, 128), F32),
    ]
    scratch += [flags((CHUNKS,))] * 8 + [flags((3, CHUNKS))] * 2 + [flags((3,))] * 2 + [flags] * 2
    scratch += [flags((4,))] * 4 + [flags((5,))] * 4 + [flags] * 2 + [flags((3,))]
    vmem = pl.BlockSpec(memory_space=pltpu.VMEM)
    density = pl.pallas_call(
        four_blocks,
        out_shape=jax.ShapeDtypeStruct((rows, width), BF16),
        in_specs=[vmem] * 3,
        out_specs=pl.BlockSpec(memory_space=pl.ANY),
        scratch_shapes=scratch,
        compiler_params=pltpu.CompilerParams(
            collective_id=0, has_side_effects=True, vmem_limit_bytes=67_000_000),
    )(
        three_index.reshape(rows, width),
        jnp.broadcast_to(occupied_energy.astype(F32)[:, None], (8, 128)),
        virtual_energy.reshape(1, width),
    )
    return density.reshape(rows, 1, width)


def solution(mesh):
    placed = (P("aux", "occ", "virt"), P("occ"), P("virt"))

    def on_device(three_index, occupied_energy, virtual_energy):
        paired = mesh.shape["occ"] == 4 and mesh.shape["aux"] == 4 and three_index.shape[1] == 1
        body = cycle_of_four if paired else any_cycle
        return body(three_index, occupied_energy, virtual_energy)

    return jax.shard_map(
        on_device, mesh=mesh, in_specs=placed, out_specs=P("aux", "occ", "virt"), check_vma=False
    )
```
